32 devices in a mesh: occ: 4 (over y, core), vir: 8 (over z, x).
Axes of the slice: x: 2, y: 2, z: 4, core: 2. Of those that a mesh axis runs over, the one named last changes fastest.
Arguments:
- amplitudes: bfloat16 [32, 16, 128, 128], P(('occ', 'vir')), may hold values from -6 to 6
- amp_slots: int32 [32, 16], P(('occ', 'vir')), may hold values from 0 to 7, as said below
- integrals: bfloat16 [64, 48, 128, 128], P('vir', 'occ'), may hold values from -0.15625 to 0.15625
- int_columns: int32 [64, 48], replicated, may hold values from 0 to 63, as said below
- slot_tile: int32 [64], replicated, may hold values from 0 to 63, each once
Outputs:
- residual: bfloat16 [32, 16, 128, 128], P(('occ', 'vir'))
The draws below stay inside these ranges and needn't reach their ends.
Inputs may be any that keep to these rules, and one draw needn't show every extreme that they name: `amp_slots`: within each group of 2 consecutive slots of a row the values are distinct. `int_columns`: the 48 entries of a row are distinct.
All inputs are finite; a program needn't handle non-finite values.
Results may differ from the reference program's by a relative error of at most 0.012.
Values may be sent and summed in bfloat16 or wider, within the bound.
A program may use at most 192 MiB of HBM per device.

```python
import jax
import jax.numpy as jnp
from jax import lax

TILE_PAIR_COUNT = 128
OWNED_VIRT_TILES = 8
OWNED_ROW_TILES = 2
VIRTUAL_TILES = 64
ROW_SLOT_COUNT = 16
INTEGRAL_ROW_NNZ = 48
OCCUPIED_ROWS = 32


def draw_amp_slots(key, part):
    row_groupings = ROW_SLOT_COUNT // OWNED_ROW_TILES
    scores = jax.random.randint(key, (OCCUPIED_ROWS, row_groupings, OWNED_VIRT_TILES), 0, 1048576) * OWNED_VIRT_TILES + jnp.arange(OWNED_VIRT_TILES, dtype=jnp.int32)
    sorted_order = jnp.argsort(scores, axis=-1, stable=True).astype(jnp.int32)
    return sorted_order[:, :, :OWNED_ROW_TILES].reshape(OCCUPIED_ROWS, ROW_SLOT_COUNT)


def draw_int_columns(key, part):
    scores = jax.random.randint(key, (VIRTUAL_TILES, VIRTUAL_TILES), 0, 1048576) * VIRTUAL_TILES + jnp.arange(VIRTUAL_TILES, dtype=jnp.int32)
    sorted_order = jnp.argsort(scores, axis=-1, stable=True).astype(jnp.int32)
    return sorted_order[:, :INTEGRAL_ROW_NNZ]


def shard_levels(key, shape, cuts, least, high):
    factor_of = 1.0
    for axis_at, shards_of in cuts:
        steps = jax.random.uniform(jax.random.fold_in(jax.random.fold_in(key, 6), axis_at), (shards_of,), jnp.float32, least / len(cuts), high / len(cuts))
        factor_of = factor_of * jnp.repeat(jnp.exp(steps), shape[axis_at] // shards_of).reshape((-1,) + (1,) * (len(shape) - 1 - axis_at))
    return factor_of


def bell_draw(rng, extent, spread, limit, cuts=(), held_as=jnp.bfloat16):
    level = shard_levels(rng, extent, cuts, -0.22, 0.18) if cuts else 1.0
    array = jax.random.normal(rng, extent, jnp.float32) * spread * level
    return jnp.minimum(jnp.maximum(array, -limit), limit).astype(held_as)


def setup_inputs(seed: int = 0) -> dict:
    arg_keys = jax.random.split(jax.random.key(seed), 6)
    amplitudes = bell_draw(arg_keys[0], (OCCUPIED_ROWS, ROW_SLOT_COUNT, TILE_PAIR_COUNT, TILE_PAIR_COUNT), 1.0, 6.0, ((0, 32),))
    amp_slots = draw_amp_slots(jax.random.fold_in(arg_keys[5], 71), 0)
    integrals = bell_draw(arg_keys[2], (VIRTUAL_TILES, INTEGRAL_ROW_NNZ, TILE_PAIR_COUNT, TILE_PAIR_COUNT), (3 * ROW_SLOT_COUNT * TILE_PAIR_COUNT // 4) ** -0.5, 0.15625, ((0, 8), (1, 4)))
    int_columns = draw_int_columns(jax.random.fold_in(arg_keys[5], 71), 0)
    slot_tile = jax.random.permutation(arg_keys[4], VIRTUAL_TILES).astype(jnp.int32)
    return dict(amplitudes=amplitudes, amp_slots=amp_slots, integrals=integrals, int_columns=int_columns, slot_tile=slot_tile)


def reference(amplitudes, amp_slots, integrals, int_columns, slot_tile):
    owner_indices = ROW_SLOT_COUNT // OWNED_ROW_TILES
    start_offsets = (jnp.arange(ROW_SLOT_COUNT, dtype=jnp.int32) // OWNED_ROW_TILES) * OWNED_VIRT_TILES

    def one_row(pair):
        row_amps, row_slots = pair
        storage = (start_offsets + row_slots).astype(jnp.int32)
        tile_identifiers = slot_tile[storage]
        picked = integrals[storage].reshape(owner_indices, OWNED_ROW_TILES, INTEGRAL_ROW_NNZ, TILE_PAIR_COUNT, TILE_PAIR_COUNT)
        columns = int_columns[storage].reshape(owner_indices, OWNED_ROW_TILES, INTEGRAL_ROW_NNZ)
        grouped = row_amps.reshape(owner_indices, OWNED_ROW_TILES, TILE_PAIR_COUNT, TILE_PAIR_COUNT)

        def owner_term(triple):
            owner_amps, owner_ints, owner_cols = triple
            prods = jnp.einsum("kpq,kjqt->kjpt", owner_amps.astype(jnp.float32), owner_ints.astype(jnp.float32), precision=lax.Precision.HIGHEST)
            matches = (owner_cols[:, :, None] == tile_identifiers[None, None, :]).astype(jnp.float32)
            summed = jnp.einsum("kjs,kjpt->spt", matches, prods, precision=lax.Precision.HIGHEST)
            return summed.astype(jnp.bfloat16)

        terms = lax.map(owner_term, (grouped, picked, columns))
        return jnp.sum(terms.astype(jnp.float32), axis=0).astype(jnp.bfloat16)

    return lax.map(one_row, (amplitudes, amp_slots))
```

```python
import functools

import jax
import jax.numpy as jnp
from jax import lax
from jax.experimental import pallas as pl
from jax.experimental.pallas import tpu as pltpu
from jax.sharding import PartitionSpec as P

MESH = pl.DeviceIdType.MESH
CORES = 2
CHUNKS = ((False, 0, 32), (False, 32, 32), (False, 64, 32), (False, 96, 32))


def jobs_of(ny, chunks):
    jobs = []
    for number, (spread, _, _) in enumerate(chunks):
        for step in range(ny if spread else 1):
            jobs.append((number, step))
    return jobs


def kernel(dims, chunks, jobs, amps, tables, ints, out, *scratch):
    ny, nz, nx, slots, tiles = dims
    nv, no = nz * nx, ny * CORES
    spread_any = any(c[0] for c in chunks)
    n_chunks, n_jobs = len(chunks), len(jobs)
    weights = scratch[:n_chunks]
    terms = scratch[n_chunks : n_chunks + n_jobs]
    from_x = scratch[n_chunks + n_jobs : n_chunks + 2 * n_jobs]
    from_z = scratch[n_chunks + 2 * n_jobs : n_chunks + 3 * n_jobs]
    from_y = scratch[n_chunks + 3 * n_jobs : n_chunks + 4 * n_jobs]
    amp_buf, tab_buf, tab_smem, send_sem, recv_sem, loc_sem = scratch[n_chunks + 4 * n_jobs :]

    occ, vir = lax.axis_index("occ"), lax.axis_index("vir")
    y, core = occ // CORES, lax.rem(occ, CORES)
    z, x = vir // nx, lax.rem(vir, nx)
    partner = y * CORES + (1 - core)

    def occ_at(step):
        return lax.rem(y + step, ny) * CORES + core

    counts = {"remote": 0, "local": 0}
    sent = []

    def remote(src, dst, where):
        at = counts["remote"]
        counts["remote"] += 1
        copy = pltpu.make_async_remote_copy(
            src_ref=src, dst_ref=dst, send_sem=send_sem.at[at], recv_sem=recv_sem.at[at],
            device_id=where, device_id_type=MESH,
        )
        copy.start()
        sent.append(copy)
        return copy

    def local(src, dst):
        at = counts["local"]
        counts["local"] += 1
        copy = pltpu.make_async_copy(src, dst, loc_sem.at[at])
        copy.start()
        return copy

    barrier = pltpu.get_barrier_semaphore()
    peers = [{"occ": occ, "vir": lax.rem(vir + d, nv)} for d in range(1, nv)]
    peers += [{"occ": occ_at(d), "vir": vir} for d in range(1, ny)]
    peers += [{"occ": partner, "vir": vir}]
    for peer in peers:
        pl.semaphore_signal(barrier, inc=1, device_id=peer, device_id_type=MESH)

    own_copies = {}

    def span(number, source):
        spread = chunks[number][0]
        first = (lax.rem(source, CORES) if spread else source) * tiles
        return weights[number].at[pl.ds(first, tiles)]

    def part(number):
        _, first, width = chunks[number]
        return ints.at[:, pl.ds(first, width), :]

    amp_own = local(amps.at[vir], amp_buf.at[0, vir])
    tab_own = local(tables.at[vir], tab_buf.at[0, vir])
    for number, (_, _, width) in enumerate(chunks):
        own_copies[number] = local(part(number), span(number, occ))
    for number, (spread, _, width) in enumerate(chunks):
        weights[number][(CORES if spread else no) * tiles] = jnp.zeros((width, 128), jnp.bfloat16)

    pl.semaphore_wait(barrier, len(peers))

    across, side = {}, {}

    def start_across(number):
        across[number] = [
            remote(part(number), span(number, occ), {"occ": occ_at(d), "vir": vir})
            for d in range(1, ny)
        ]

    def start_side(number):
        side[number] = [remote(part(number), span(number, occ), {"occ": partner, "vir": vir})]

    narrow = [c for c in range(n_chunks) if not chunks[c][0]]
    incoming = []
    for d in range(1, nv):
        to = lax.rem(vir + d, nv)
        incoming.append(remote(tables.at[to], tab_buf.at[0, vir], {"occ": occ, "vir": to}))
        incoming.append(remote(amps.at[to], amp_buf.at[0, vir], {"occ": occ, "vir": to}))
    start_across(narrow[0])
    for number in range(n_chunks):
        start_side(number)
    if not spread_any:
        for number in narrow[1:]:
            start_across(number)
    amp_own.wait()
    tab_own.wait()
    for copy in incoming:
        copy.wait_recv()
    others = []
    if spread_any:
        for d in range(1, ny):
            where = {"occ": occ_at(d), "vir": vir}
            others.append(
                (
                    remote(tab_buf.at[0], tab_buf.at[d], where),
                    remote(amp_buf.at[0], amp_buf.at[d], where),
                )
            )
        for number in narrow[1:]:
            start_across(number)
    tab_copy = local(tab_buf.at[0], tab_smem.at[0])
    tab_copy.wait()

    def gather(number):
        own_copies[number].wait()
        if not chunks[number][0]:
            for d in range(1, ny):
                across[number][d - 1].wait_recv()
                source = lax.rem(y - d + ny, ny) * CORES + core
                side[number].append(
                    remote(span(number, source), span(number, source), {"occ": partner, "vir": vir})
                )
        for copy in side[number]:
            copy.wait_recv()

    def compute(job, x_to):
        number, step = jobs[job]
        spread, _, width = chunks[number]
        weight, term = weights[number], terms[job]
        group = step
        per_slot = amp_buf.shape[2] // 128

        def row(z_to, carry):
            r = z_to * nx + x_to
            columns = []
            for k in range(per_slot):
                pieces = []
                for s in range(slots):
                    at = tab_smem[group, r, k, s]
                    if spread:
                        at = at - y * (CORES * tiles)
                        good = (at >= 0) & (at < CORES * tiles)
                        at = jnp.where(good, at, CORES * tiles)
                    pieces.append(weight[at])
                columns.append(jnp.concatenate(pieces, axis=0))
            left = jnp.concatenate(columns, axis=1)
            prod = jnp.dot(left, amp_buf[group, r], preferred_element_type=jnp.float32)
            term[x_to, z_to] = prod.astype(jnp.bfloat16).reshape(slots, width, 128)
            return carry

        lax.fori_loop(0, nz, row, 0)

    x_copies, z_copies, y_copies = {}, {}, {}

    def first_stage(job):
        x_copies[job] = []
        for d in range(1, nx):
            to = lax.rem(x + d, nx)
            compute(job, to)
            x_copies[job].append(
                remote(terms[job].at[to], from_x[job].at[d - 1], {"occ": occ, "vir": z * nx + to})
            )
        compute(job, x)

    def second_stage(job):
        for copy in x_copies[job]:
            copy.wait_recv()
        z_copies[job] = []
        for d in range(1, nz + 1):
            to = lax.rem(z + d, nz)
            total = terms[job][x, to].astype(jnp.float32)
            for e in range(nx - 1):
                total += from_x[job][e, to].astype(jnp.float32)
            terms[job][x, to] = total.astype(jnp.bfloat16)
            if d < nz:
                z_copies[job].append(
                    remote(
                        terms[job].at[x, to], from_z[job].at[d - 1],
                        {"occ": occ, "vir": to * nx + x},
                    )
                )

    def third_stage(job):
        number, step = jobs[job]
        spread, first, width = chunks[number]
        for copy in z_copies[job]:
            copy.wait_recv()
        total = terms[job][x, z].astype(jnp.float32)
        for e in range(nz - 1):
            total += from_z[job][e].astype(jnp.float32)
        if step > 0:
            terms[job][x, z] = total.astype(jnp.bfloat16)
            y_copies[job] = remote(
                terms[job].at[x, z], from_y[job], {"occ": occ_at(step), "vir": vir}
            )
            return
        for other in range(n_jobs):
            if jobs[other][0] == number and jobs[other][1] > 0:
                y_copies[other].wait_recv()
                total += from_y[other][...].astype(jnp.float32)
        out[:, pl.ds(first, width), :] = total.astype(jnp.bfloat16)

    if spread_any:
        order = [j for j in range(n_jobs) if jobs[j][1] == 0 and chunks[jobs[j][0]][0]]
        order += [j for j in range(n_jobs) if not chunks[jobs[j][0]][0]]
        late = [j for j in range(n_jobs) if jobs[j][1] > 0]
        order = order[:2] + late + order[2:]
    else:
        order = list(range(n_jobs))
    gathered = set()
    finals = []

    def flush(job):
        if chunks[jobs[job][0]][0] and jobs[job][1] == 0:
            finals.append(job)
        else:
            third_stage(job)

    previous = None
    for job in order:
        number, step = jobs[job]
        if number not in gathered:
            gathered.add(number)
            gather(number)
        if step > 0:
            for copy in others[step - 1]:
                copy.wait_recv()
            again = local(tab_buf.at[step], tab_smem.at[step])
            again.wait()
        first_stage(job)
        if previous is not None:
            flush(previous)
        second_stage(job)
        previous = job
    flush(previous)
    for job in finals:
        third_stage(job)
    for copy in sent:
        copy.wait_send()


def body(nx, amplitudes, amp_slots, integrals, int_columns, slot_tile):
    _, slots, tile, _ = amplitudes.shape
    nv, no = lax.axis_size("vir"), lax.axis_size("occ")
    ny, nz = no // CORES, nv // nx
    owned, share = integrals.shape[:2]
    tiles = owned * share
    per_owner = slots // nv
    chunks = CHUNKS if ny == 2 else tuple((False, first, width) for _, first, width in CHUNKS)
    jobs = jobs_of(ny, chunks)

    here = amp_slots[0]
    store = (jnp.arange(slots, dtype=jnp.int32) // per_owner) * owned + here
    hot = store[:, None] == jnp.arange(nv * owned, dtype=jnp.int32)[None, :]
    tile_id = jnp.sum(jnp.where(hot, slot_tile[None, :], 0), axis=1)
    columns = jnp.sum(jnp.where(hot[:, :, None], int_columns[None], 0), axis=1)
    entry = jnp.arange(share * no, dtype=jnp.int32)
    place = (entry // share) * tiles + entry % share
    match = columns[:, :, None] == tile_id[None, None, :]
    place = place[None, :, None] + (here * share)[:, None, None]
    table = jnp.min(jnp.where(match, place, no * tiles), axis=1)
    table = table.reshape(nv, per_owner, slots)
    table = jnp.pad(table, ((0, 0), (0, 8 - per_owner), (0, 128 - slots)))

    amps = jnp.swapaxes(amplitudes[0], 1, 2).reshape(nv, per_owner * tile, tile)
    ints = jnp.swapaxes(integrals, 2, 3).reshape(tiles, tile, tile)

    bf16 = jnp.bfloat16
    groups = ny if any(c[0] for c in chunks) else 1
    scratch = [
        pltpu.VMEM(((CORES if spread else no) * tiles + 1, width, tile), bf16)
        for spread, _, width in chunks
    ]
    widths = [chunks[number][2] for number, _ in jobs]
    scratch += [pltpu.VMEM((nx, nz, slots, w, tile), bf16) for w in widths]
    scratch += [pltpu.VMEM((nx - 1, nz, slots, w, tile), bf16) for w in widths]
    scratch += [pltpu.VMEM((nz - 1, slots, w, tile), bf16) for w in widths]
    scratch += [
        pltpu.VMEM((slots, w, tile) if step > 0 else (8, 128), bf16)
        for w, (_, step) in zip(widths, jobs)
    ]
    scratch += [
        pltpu.VMEM((groups, nv, per_owner * tile, tile), bf16),
        pltpu.VMEM((groups, nv, 8, 128), jnp.int32),
        pltpu.SMEM((groups, nv, 8, 128), jnp.int32),
        pltpu.SemaphoreType.DMA((128,)),
        pltpu.SemaphoreType.DMA((128,)),
        pltpu.SemaphoreType.DMA((16,)),
    ]
    result = pl.pallas_call(
        functools.partial(kernel, (ny, nz, nx, slots, tiles), chunks, jobs),
        out_shape=jax.ShapeDtypeStruct((slots, tile, tile), bf16),
        in_specs=[pl.BlockSpec(memory_space=pl.ANY)] * 3,
        out_specs=pl.BlockSpec(memory_space=pltpu.VMEM),
        scratch_shapes=scratch,
        compiler_params=pltpu.CompilerParams(
            collective_id=0, has_side_effects=True, vmem_limit_bytes=66_000_000
        ),
    )(amps, table, ints)
    return jnp.swapaxes(result, 1, 2)[None]


def solution(mesh):
    nv = mesh.shape["vir"]
    nx = nv // min(4, nv)
    in_specs = (
        P(("occ", "vir"), None, None, None),
        P(("occ", "vir"), None),
        P("vir", "occ", None, None),
        P(),
        P(),
    )
    out_specs = P(("occ", "vir"), None, None, None)
    return jax.shard_map(
        functools.partial(body, nx), mesh=mesh, in_specs=in_specs, out_specs=out_specs,
        check_vma=False,
    )
```

```python
import functools

import jax
import jax.numpy as jnp
from jax import lax
from jax.experimental import pallas as pl
from jax.experimental.pallas import tpu as pltpu
from jax.sharding import PartitionSpec as P

MESH = pl.DeviceIdType.MESH
CORES = 2
CHUNKS = ((False, 0, 32), (False, 32, 32), (False, 64, 32), (False, 96, 16), (False, 112, 16))


def jobs_of(ny, chunks):
    jobs = []
    for number, (spread, _, _) in enumerate(chunks):
        for step in range(ny if spread else 1):
            jobs.append((number, step))
    return jobs


def kernel(dims, chunks, jobs, own_slots, slot_tile, columns_of, amps_in, ints, out, *scratch):
    ny, nz, nx, slots, owned, share = dims
    tiles = owned * share
    nv, no = nz * nx, ny * CORES
    spread_any = any(c[0] for c in chunks)
    n_chunks, n_jobs = len(chunks), len(jobs)
    weights = scratch[:n_chunks]
    terms = scratch[n_chunks : n_chunks + n_jobs]
    from_x = scratch[n_chunks + n_jobs : n_chunks + 2 * n_jobs]
    from_z = scratch[n_chunks + 2 * n_jobs : n_chunks + 3 * n_jobs]
    from_y = scratch[n_chunks + 3 * n_jobs : n_chunks + 4 * n_jobs]
    raw_ints, raw_amps, amps, tables, amp_buf, tab_buf, tab_smem, send_sem, recv_sem, loc_sem = scratch[n_chunks + 4 * n_jobs :]

    occ, vir = lax.axis_index("occ"), lax.axis_index("vir")
    y, core = occ // CORES, lax.rem(occ, CORES)
    z, x = vir // nx, lax.rem(vir, nx)
    partner = y * CORES + (1 - core)

    def occ_at(step):
        return lax.rem(y + step, ny) * CORES + core

    counts = {"remote": 0, "local": 0}
    sent = []

    def remote(src, dst, where):
        at = counts["remote"]
        counts["remote"] += 1
        copy = pltpu.make_async_remote_copy(
            src_ref=src, dst_ref=dst, send_sem=send_sem.at[at], recv_sem=recv_sem.at[at],
            device_id=where, device_id_type=MESH,
        )
        copy.start()
        sent.append(copy)
        return copy

    def local(src, dst):
        at = counts["local"]
        counts["local"] += 1
        copy = pltpu.make_async_copy(src, dst, loc_sem.at[at])
        copy.start()
        return copy

    barrier = pltpu.get_barrier_semaphore()
    peers = [{"occ": occ, "vir": lax.rem(vir + d, nv)} for d in range(1, nv)]
    peers += [{"occ": occ_at(d), "vir": vir} for d in range(1, ny)]
    peers += [{"occ": partner, "vir": vir}]
    for peer in peers:
        pl.semaphore_signal(barrier, inc=1, device_id=peer, device_id_type=MESH)

    held = raw_ints.shape[0] // share

    def fetch(g):
        return local(
            ints.at[pl.ds(g * share, share)], raw_ints.at[pl.ds((g % held) * share, share)]
        )

    pieces_in = [fetch(g) for g in range(held)]
    amps_copy = local(amps_in, raw_amps)

    def span(number, source):
        spread = chunks[number][0]
        first = (lax.rem(source, CORES) if spread else source) * tiles
        return weights[number].at[pl.ds(first, tiles)]

    for number, (spread, _, width) in enumerate(chunks):
        weights[number][(CORES if spread else no) * tiles] = jnp.zeros((width, 128), jnp.bfloat16)

    def turn(slot, tile):
        turned = raw_ints[slot].T
        for number, (spread, first, width) in enumerate(chunks):
            at = (core if spread else occ) * tiles + tile
            weights[number][at] = turned[first : first + width]

    across, side = {}, {}

    def start_across(number):
        across[number] = [
            remote(span(number, occ), span(number, occ), {"occ": occ_at(d), "vir": vir})
            for d in range(1, ny)
        ]

    def start_side(number):
        side[number] = [
            remote(span(number, occ), span(number, occ), {"occ": partner, "vir": vir})
        ]

    narrow = [c for c in range(n_chunks) if not chunks[c][0]]
    lead = narrow[0]
    across[lead] = []

    def start_lead(g):
        piece = weights[lead].at[pl.ds(occ * tiles + g * share, share)]
        for d in range(1, ny):
            across[lead].append(remote(piece, piece, {"occ": occ_at(d), "vir": vir}))

    for g in range(owned):
        pieces_in[g].wait()

        @pl.loop(0, share)
        def _(j, g=g):
            turn((g % held) * share + j, g * share + j)

        if g + held < owned:
            pieces_in.append(fetch(g + held))

        if g == 0:
            pl.semaphore_wait(barrier, len(peers))
        else:
            start_lead(g - 1)
    start_lead(owned - 1)

    if not spread_any:
        for number in narrow[1:]:
            start_across(number)

    nv_slots = slots // nv
    rows = lax.broadcasted_iota(jnp.int32, (slots, share * no), 0)
    entry = lax.broadcasted_iota(jnp.int32, (slots, share * no), 1)
    place = (entry // share) * tiles + lax.rem(entry, share)
    wanted = jnp.zeros((slots, share * no), jnp.int32)
    for s in range(slots):
        wanted = jnp.where(rows == s, slot_tile[(s // nv_slots) * owned + own_slots[0, s]], wanted)
    lanes = lax.broadcasted_iota(jnp.int32, (slots, 128), 1)
    for v in range(nv):
        mapped = jnp.zeros((slots, 128), jnp.int32)
        for k in range(nv_slots):
            mine = own_slots[0, v * nv_slots + k]
            reached = columns_of[pl.ds(v * owned + mine, 1), :]
            found = jnp.where(reached == wanted, place + mine * share, no * tiles)
            mapped = jnp.where(lanes == k, jnp.min(found, axis=1, keepdims=True), mapped)
        tables[v] = mapped

    amps_copy.wait()

    @pl.loop(0, slots)
    def _(s):
        at = pl.ds(pl.multiple_of(lax.rem(s, nv_slots) * 128, 128), 128)
        amps[s // nv_slots, at, :] = raw_amps[s].T

    tab_own = local(tables.at[vir], tab_buf.at[0, vir])
    amp_own = local(amps.at[vir], amp_buf.at[0, vir])
    incoming = []
    for d in range(1, nv):
        to = lax.rem(vir + d, nv)
        incoming.append(remote(tables.at[to], tab_buf.at[0, vir], {"occ": occ, "vir": to}))
        incoming.append(remote(amps.at[to], amp_buf.at[0, vir], {"occ": occ, "vir": to}))
    for number in range(n_chunks):
        start_side(number)
    amp_own.wait()
    tab_own.wait()
    for copy in incoming:
        copy.wait_recv()
    others = []
    if spread_any:
        for d in range(1, ny):
            where = {"occ": occ_at(d), "vir": vir}
            others.append(
                (
                    remote(tab_buf.at[0], tab_buf.at[d], where),
                    remote(amp_buf.at[0], amp_buf.at[d], where),
                )
            )
        for number in narrow[1:]:
            start_across(number)
    tab_copy = local(tab_buf.at[0], tab_smem.at[0])
    tab_copy.wait()

    def gather(number):
        if not chunks[number][0]:
            for d in range(1, ny):
                if number == lead:
                    for g in range(owned):
                        across[number][g * (ny - 1) + d - 1].wait_recv()
                else:
                    across[number][d - 1].wait_recv()
                source = lax.rem(y - d + ny, ny) * CORES + core
                side[number].append(
                    remote(span(number, source), span(number, source), {"occ": partner, "vir": vir})
                )
        for copy in side[number]:
            copy.wait_recv()

    def compute(job, x_to):
        number, step = jobs[job]
        spread, _, width = chunks[number]
        weight, term = weights[number], terms[job]
        group = step
        per_slot = amp_buf.shape[2] // 128

        def row(z_to, carry):
            r = z_to * nx + x_to
            columns = []
            for k in range(per_slot):
                pieces = []
                for s in range(slots):
                    at = tab_smem[group, r, s, k]
                    if spread:
                        at = at - y * (CORES * tiles)
                        good = (at >= 0) & (at < CORES * tiles)
                        at = jnp.where(good, at, CORES * tiles)
                    pieces.append(weight[at])
                columns.append(jnp.concatenate(pieces, axis=0))
            left = jnp.concatenate(columns, axis=1)
            prod = jnp.dot(left, amp_buf[group, r], preferred_element_type=jnp.float32)
            term[x_to, z_to] = prod.astype(jnp.bfloat16).reshape(slots, width, 128)
            return carry

        lax.fori_loop(0, nz, row, 0)

    x_copies, z_copies, y_copies = {}, {}, {}

    def first_stage(job):
        x_copies[job] = []
        for d in range(1, nx):
            to = lax.rem(x + d, nx)
            compute(job, to)
            x_copies[job].append(
                remote(terms[job].at[to], from_x[job].at[d - 1], {"occ": occ, "vir": z * nx + to})
            )
        compute(job, x)

    def second_stage(job):
        for copy in x_copies[job]:
            copy.wait_recv()
        z_copies[job] = []
        for d in range(1, nz + 1):
            to = lax.rem(z + d, nz)
            total = terms[job][x, to].astype(jnp.float32)
            for e in range(nx - 1):
                total += from_x[job][e, to].astype(jnp.float32)
            terms[job][x, to] = total.astype(jnp.bfloat16)
            if d < nz:
                z_copies[job].append(
                    remote(
                        terms[job].at[x, to], from_z[job].at[d - 1],
                        {"occ": occ, "vir": to * nx + x},
                    )
                )

    def third_stage(job):
        number, step = jobs[job]
        spread, first, width = chunks[number]
        for copy in z_copies[job]:
            copy.wait_recv()
        total = terms[job][x, z].astype(jnp.float32)
        for e in range(nz - 1):
            total += from_z[job][e].astype(jnp.float32)
        if step > 0:
            terms[job][x, z] = total.astype(jnp.bfloat16)
            y_copies[job] = remote(
                terms[job].at[x, z], from_y[job], {"occ": occ_at(step), "vir": vir}
            )
            return
        for other in range(n_jobs):
            if jobs[other][0] == number and jobs[other][1] > 0:
                y_copies[other].wait_recv()
                total += from_y[other][...].astype(jnp.float32)
        out[:, pl.ds(first, width), :] = total.astype(jnp.bfloat16)

    if spread_any:
        order = [j for j in range(n_jobs) if jobs[j][1] == 0 and chunks[jobs[j][0]][0]]
        order += [j for j in range(n_jobs) if not chunks[jobs[j][0]][0]]
        late = [j for j in range(n_jobs) if jobs[j][1] > 0]
        order = order[:2] + late + order[2:]
    else:
        order = list(range(n_jobs))
    gathered = set()
    finals = []

    def flush(job):
        if chunks[jobs[job][0]][0] and jobs[job][1] == 0:
            finals.append(job)
        else:
            third_stage(job)

    previous = None
    for job in order:
        number, step = jobs[job]
        if number not in gathered:
            gathered.add(number)
            gather(number)
        if step > 0:
            for copy in others[step - 1]:
                copy.wait_recv()
            again = local(tab_buf.at[step], tab_smem.at[step])
            again.wait()
        first_stage(job)
        if previous is not None:
            flush(previous)
        second_stage(job)
        previous = job
    flush(previous)
    for job in finals:
        third_stage(job)
    for copy in sent:
        copy.wait_send()


def body(nx, amplitudes, amp_slots, integrals, int_columns, slot_tile):
    _, slots, tile, _ = amplitudes.shape
    nv, no = lax.axis_size("vir"), lax.axis_size("occ")
    ny, nz = no // CORES, nv // nx
    owned, share = integrals.shape[:2]
    tiles = owned * share
    per_owner = slots // nv
    chunks = CHUNKS if ny == 2 else tuple((False, first, width) for _, first, width in CHUNKS)
    jobs = jobs_of(ny, chunks)

    ints = integrals.reshape(tiles, tile, tile)

    bf16 = jnp.bfloat16
    groups = ny if any(c[0] for c in chunks) else 1
    scratch = [
        pltpu.VMEM(((CORES if spread else no) * tiles + 1, width, tile), bf16)
        for spread, _, width in chunks
    ]
    widths = [chunks[number][2] for number, _ in jobs]
    scratch += [pltpu.VMEM((nx, nz, slots, w, tile), bf16) for w in widths]
    scratch += [pltpu.VMEM((nx - 1, nz, slots, w, tile), bf16) for w in widths]
    scratch += [pltpu.VMEM((nz - 1, slots, w, tile), bf16) for w in widths]
    scratch += [
        pltpu.VMEM((slots, w, tile) if step > 0 else (8, 128), bf16)
        for w, (_, step) in zip(widths, jobs)
    ]
    scratch += [
        pltpu.VMEM((min(4, owned) * share, tile, tile), bf16),
        pltpu.VMEM((slots, tile, tile), bf16),
        pltpu.VMEM((nv, per_owner * tile, tile), bf16),
        pltpu.VMEM((nv, slots, 128), jnp.int32),
        pltpu.VMEM((groups, nv, per_owner * tile, tile), bf16),
        pltpu.VMEM((groups, nv, slots, 128), jnp.int32),
        pltpu.SMEM((groups, nv, slots, 128), jnp.int32),
        pltpu.SemaphoreType.DMA((128,)),
        pltpu.SemaphoreType.DMA((128,)),
        pltpu.SemaphoreType.DMA((32,)),
    ]
    result = pl.pallas_call(
        functools.partial(kernel, (ny, nz, nx, slots, owned, share), chunks, jobs),
        out_shape=jax.ShapeDtypeStruct((slots, tile, tile), bf16),
        in_specs=[
            pl.BlockSpec(memory_space=pltpu.SMEM),
            pl.BlockSpec(memory_space=pltpu.SMEM),
            pl.BlockSpec(memory_space=pltpu.VMEM),
            pl.BlockSpec(memory_space=pl.ANY),
            pl.BlockSpec(memory_space=pl.ANY),
        ],
        out_specs=pl.BlockSpec(memory_space=pltpu.VMEM),
        scratch_shapes=scratch,
        compiler_params=pltpu.CompilerParams(
            collective_id=0, has_side_effects=True, vmem_limit_bytes=66_000_000
        ),
    )(amp_slots, slot_tile, int_columns, amplitudes[0], ints)
    return jnp.swapaxes(result, 1, 2)[None]


def solution(mesh):
    nv = mesh.shape["vir"]
    nx = nv // min(4, nv)
    in_specs = (
        P(("occ", "vir"), None, None, None),
        P(("occ", "vir"), None),
        P("vir", "occ", None, None),
        P(),
        P(),
    )
    out_specs = P(("occ", "vir"), None, None, None)
    return jax.shard_map(
        functools.partial(body, nx), mesh=mesh, in_specs=in_specs, out_specs=out_specs,
        check_vma=False,
    )
```

```python
import functools

import jax
import jax.numpy as jnp
from jax import lax
from jax.experimental import pallas as pl
from jax.experimental.pallas import tpu as pltpu
from jax.sharding import PartitionSpec as P

MESH = pl.DeviceIdType.MESH
CORES = 2
CHUNKS = tuple((False, 16 * i, 16) for i in range(8))


def jobs_of(ny, chunks):
    jobs = []
    for number, (spread, _, _) in enumerate(chunks):
        for step in range(ny if spread else 1):
            jobs.append((number, step))
    return jobs


def events_of(chunks, jobs):
    spread = [j for j, (c, _) in enumerate(jobs) if chunks[c][0]]
    plain = [j for j, (c, _) in enumerate(jobs) if not chunks[c][0]]
    order = spread[:1] + plain[:1] + spread[1:] + plain[1:]
    events = []
    count = len(order)
    for at in range(count + 2):
        for stage, back in ((1, 0), (2, 1), (3, 2)):
            if 0 <= at - back < count and not (stage == 3 and order[at - back] in spread[:1]):
                events.append((stage, order[at - back]))
    return events + [(3, one) for one in spread[:1]]


def kernel(dims, chunks, jobs, events, own_slots, slot_tile, columns_of, amps_in, ints, out, *scratch):
    ny, nz, nx, slots, owned, share = dims
    tiles = owned * share
    nv, no = nz * nx, ny * CORES
    spread_any = any(c[0] for c in chunks)
    n_chunks, n_jobs = len(chunks), len(jobs)
    weights = scratch[:n_chunks]
    terms = scratch[n_chunks : n_chunks + n_jobs]
    from_x = scratch[n_chunks + n_jobs : n_chunks + 2 * n_jobs]
    from_z = scratch[n_chunks + 2 * n_jobs : n_chunks + 3 * n_jobs]
    from_y = scratch[n_chunks + 3 * n_jobs : n_chunks + 4 * n_jobs]
    raw_ints, raw_amps, amps, tables, amp_buf, tab_buf, tab_smem, send_sem, recv_sem, loc_sem = scratch[n_chunks + 4 * n_jobs :]

    occ, vir = lax.axis_index("occ"), lax.axis_index("vir")
    y, core = occ // CORES, lax.rem(occ, CORES)
    z, x = vir // nx, lax.rem(vir, nx)
    partner = y * CORES + (1 - core)

    def occ_at(step):
        return lax.rem(y + step, ny) * CORES + core

    counts = {"remote": 0, "local": 0}
    sent = []

    def remote(src, dst, where):
        at = counts["remote"]
        counts["remote"] += 1
        copy = pltpu.make_async_remote_copy(
            src_ref=src, dst_ref=dst, send_sem=send_sem.at[at], recv_sem=recv_sem.at[at],
            device_id=where, device_id_type=MESH,
        )
        copy.start()
        sent.append(copy)
        return copy

    def local(src, dst):
        at = counts["local"]
        counts["local"] += 1
        copy = pltpu.make_async_copy(src, dst, loc_sem.at[at])
        copy.start()
        return copy

    barrier = pltpu.get_barrier_semaphore()
    peers = [{"occ": occ, "vir": lax.rem(vir + d, nv)} for d in range(1, nv)]
    peers += [{"occ": occ_at(d), "vir": vir} for d in range(1, ny)]
    peers += [{"occ": partner, "vir": vir}]
    for peer in peers:
        pl.semaphore_signal(barrier, inc=1, device_id=peer, device_id_type=MESH)

    held = raw_ints.shape[0] // share

    def fetch(g):
        return local(
            ints.at[pl.ds(g * share, share)], raw_ints.at[pl.ds((g % held) * share, share)]
        )

    pieces_in = [fetch(g) for g in range(held)]
    amps_copy = local(amps_in, raw_amps)

    def span(number, source):
        spread = chunks[number][0]
        first = (lax.rem(source, CORES) if spread else source) * tiles
        return weights[number].at[pl.ds(first, tiles)]

    for number, (spread, _, width) in enumerate(chunks):
        weights[number][(CORES if spread else no) * tiles] = jnp.zeros((width, 128), jnp.bfloat16)

    def turn(slot, tile):
        turned = raw_ints[slot].T
        for number, (spread, first, width) in enumerate(chunks):
            at = (core if spread else occ) * tiles + tile
            weights[number][at] = turned[first : first + width]

    across, side = {}, {}

    def start_across(number):
        across[number] = [
            remote(span(number, occ), span(number, occ), {"occ": occ_at(d), "vir": vir})
            for d in range(1, ny)
        ]

    def start_side(number):
        side[number] = [
            remote(span(number, occ), span(number, occ), {"occ": partner, "vir": vir})
        ]

    narrow = [c for c in range(n_chunks) if not chunks[c][0]]
    lead = narrow[0]
    across[lead] = []

    def start_lead(g):
        piece = weights[lead].at[pl.ds(occ * tiles + g * share, share)]
        for d in range(1, ny):
            across[lead].append(remote(piece, piece, {"occ": occ_at(d), "vir": vir}))

    for g in range(owned):
        pieces_in[g].wait()

        @pl.loop(0, share)
        def _(j, g=g):
            turn((g % held) * share + j, g * share + j)

        if g + held < owned:
            pieces_in.append(fetch(g + held))

        if g == 0:
            pl.semaphore_wait(barrier, len(peers))
        else:
            start_lead(g - 1)
    start_lead(owned - 1)

    if not spread_any:
        for number in narrow[1:]:
            start_across(number)

    nv_slots = slots // nv
    rows = lax.broadcasted_iota(jnp.int32, (slots, share * no), 0)
    entry = lax.broadcasted_iota(jnp.int32, (slots, share * no), 1)
    place = (entry // share) * tiles + lax.rem(entry, share)
    wanted = jnp.zeros((slots, share * no), jnp.int32)
    for s in range(slots):
        wanted = jnp.where(rows == s, slot_tile[(s // nv_slots) * owned + own_slots[0, s]], wanted)
    lanes = lax.broadcasted_iota(jnp.int32, (slots, 128), 1)
    for v in range(nv):
        mapped = jnp.zeros((slots, 128), jnp.int32)
        for k in range(nv_slots):
            mine = own_slots[0, v * nv_slots + k]
            reached = columns_of[pl.ds(v * owned + mine, 1), :]
            found = jnp.where(reached == wanted, place + mine * share, no * tiles)
            mapped = jnp.where(lanes == k, jnp.min(found, axis=1, keepdims=True), mapped)
        tables[v] = mapped

    amps_copy.wait()

    @pl.loop(0, slots)
    def _(s):
        at = pl.ds(pl.multiple_of(lax.rem(s, nv_slots) * 128, 128), 128)
        amps[s // nv_slots, at, :] = raw_amps[s].T

    tab_own = local(tables.at[vir], tab_buf.at[0, vir])
    amp_own = local(amps.at[vir], amp_buf.at[0, vir])
    incoming = []
    for d in range(1, nv):
        to = lax.rem(vir + d, nv)
        incoming.append(remote(tables.at[to], tab_buf.at[0, vir], {"occ": occ, "vir": to}))
        incoming.append(remote(amps.at[to], amp_buf.at[0, vir], {"occ": occ, "vir": to}))
    for number in range(n_chunks):
        start_side(number)
    amp_own.wait()
    tab_own.wait()
    for copy in incoming:
        copy.wait_recv()
    others = []
    if spread_any:
        for d in range(1, ny):
            where = {"occ": occ_at(d), "vir": vir}
            others.append(
                (
                    remote(tab_buf.at[0], tab_buf.at[d], where),
                    remote(amp_buf.at[0], amp_buf.at[d], where),
                )
            )
        for number in narrow[1:]:
            start_across(number)
    tab_copy = local(tab_buf.at[0], tab_smem.at[0])
    tab_copy.wait()

    def gather(number):
        if not chunks[number][0]:
            for d in range(1, ny):
                if number == lead:
                    for g in range(owned):
                        across[number][g * (ny - 1) + d - 1].wait_recv()
                else:
                    across[number][d - 1].wait_recv()
                source = lax.rem(y - d + ny, ny) * CORES + core
                side[number].append(
                    remote(span(number, source), span(number, source), {"occ": partner, "vir": vir})
                )
        for copy in side[number]:
            copy.wait_recv()

    def compute(job, x_to):
        number, step = jobs[job]
        spread, _, width = chunks[number]
        weight, term = weights[number], terms[job]
        group = step
        per_slot = amp_buf.shape[2] // 128

        def row(z_to, carry):
            r = z_to * nx + x_to
            columns = []
            for k in range(per_slot):
                pieces = []
                for s in range(slots):
                    at = tab_smem[group, r, s, k]
                    if spread:
                        at = at - y * (CORES * tiles)
                        good = (at >= 0) & (at < CORES * tiles)
                        at = jnp.where(good, at, CORES * tiles)
                    pieces.append(weight[at])
                columns.append(jnp.concatenate(pieces, axis=0))
            left = jnp.concatenate(columns, axis=1)
            prod = jnp.dot(left, amp_buf[group, r], preferred_element_type=jnp.float32)
            term[x_to, z_to] = prod.astype(jnp.bfloat16).reshape(slots, width, 128)
            return carry

        lax.fori_loop(0, nz, row, 0)

    x_copies, z_copies, y_copies = {}, {}, {}

    def first_stage(job):
        x_copies[job] = []
        for d in range(1, nx):
            to = lax.rem(x + d, nx)
            compute(job, to)
            x_copies[job].append(
                remote(terms[job].at[to], from_x[job].at[d - 1], {"occ": occ, "vir": z * nx + to})
            )
        compute(job, x)

    def second_stage(job):
        for copy in x_copies[job]:
            copy.wait_recv()
        z_copies[job] = []
        for d in range(1, nz + 1):
            to = lax.rem(z + d, nz)
            total = terms[job][x, to].astype(jnp.float32)
            for e in range(nx - 1):
                total += from_x[job][e, to].astype(jnp.float32)
            terms[job][x, to] = total.astype(jnp.bfloat16)
            if d < nz:
                z_copies[job].append(
                    remote(
                        terms[job].at[x, to], from_z[job].at[d - 1],
                        {"occ": occ, "vir": to * nx + x},
                    )
                )

    def third_stage(job):
        number, step = jobs[job]
        spread, first, width = chunks[number]
        for copy in z_copies[job]:
            copy.wait_recv()
        total = terms[job][x, z].astype(jnp.float32)
        for e in range(nz - 1):
            total += from_z[job][e].astype(jnp.float32)
        if step > 0:
            terms[job][x, z] = total.astype(jnp.bfloat16)
            y_copies[job] = remote(
                terms[job].at[x, z], from_y[job], {"occ": occ_at(step), "vir": vir}
            )
            return
        for other in range(n_jobs):
            if jobs[other][0] == number and jobs[other][1] > 0:
                y_copies[other].wait_recv()
                total += from_y[other][...].astype(jnp.float32)
        out[:, pl.ds(first, width), :] = total.astype(jnp.bfloat16)

    gathered = set()
    for stage, job in events:
        number, step = jobs[job]
        if stage == 1:
            if number not in gathered:
                gathered.add(number)
                gather(number)
            if step > 0:
                for copy in others[step - 1]:
                    copy.wait_recv()
                local(tab_buf.at[step], tab_smem.at[step]).wait()
            first_stage(job)
        elif stage == 2:
            second_stage(job)
        else:
            third_stage(job)
    for copy in sent:
        copy.wait_send()


def body(nx, amplitudes, amp_slots, integrals, int_columns, slot_tile):
    _, slots, tile, _ = amplitudes.shape
    nv, no = lax.axis_size("vir"), lax.axis_size("occ")
    ny, nz = no // CORES, nv // nx
    owned, share = integrals.shape[:2]
    tiles = owned * share
    per_owner = slots // nv
    chunks = CHUNKS if ny == 2 else tuple((False, first, width) for _, first, width in CHUNKS)
    jobs = jobs_of(ny, chunks)

    ints = integrals.reshape(tiles, tile, tile)

    bf16 = jnp.bfloat16
    groups = ny if any(c[0] for c in chunks) else 1
    scratch = [
        pltpu.VMEM(((CORES if spread else no) * tiles + 1, width, tile), bf16)
        for spread, _, width in chunks
    ]
    widths = [chunks[number][2] for number, _ in jobs]
    scratch += [pltpu.VMEM((nx, nz, slots, w, tile), bf16) for w in widths]
    scratch += [pltpu.VMEM((nx - 1, nz, slots, w, tile), bf16) for w in widths]
    scratch += [pltpu.VMEM((nz - 1, slots, w, tile), bf16) for w in widths]
    scratch += [
        pltpu.VMEM((slots, w, tile) if step > 0 else (8, 128), bf16)
        for w, (_, step) in zip(widths, jobs)
    ]
    scratch += [
        pltpu.VMEM((min(4, owned) * share, tile, tile), bf16),
        pltpu.VMEM((slots, tile, tile), bf16),
        pltpu.VMEM((nv, per_owner * tile, tile), bf16),
        pltpu.VMEM((nv, slots, 128), jnp.int32),
        pltpu.VMEM((groups, nv, per_owner * tile, tile), bf16),
        pltpu.VMEM((groups, nv, slots, 128), jnp.int32),
        pltpu.SMEM((groups, nv, slots, 128), jnp.int32),
        pltpu.SemaphoreType.DMA((128,)),
        pltpu.SemaphoreType.DMA((128,)),
        pltpu.SemaphoreType.DMA((32,)),
    ]
    result = pl.pallas_call(
        functools.partial(kernel, (ny, nz, nx, slots, owned, share), chunks, jobs, events_of(chunks, jobs)),
        out_shape=jax.ShapeDtypeStruct((slots, tile, tile), bf16),
        in_specs=[
            pl.BlockSpec(memory_space=pltpu.SMEM),
            pl.BlockSpec(memory_space=pltpu.SMEM),
            pl.BlockSpec(memory_space=pltpu.VMEM),
            pl.BlockSpec(memory_space=pl.ANY),
            pl.BlockSpec(memory_space=pl.ANY),
        ],
        out_specs=pl.BlockSpec(memory_space=pltpu.VMEM),
        scratch_shapes=scratch,
        compiler_params=pltpu.CompilerParams(
            collective_id=0, has_side_effects=True, vmem_limit_bytes=66_000_000
        ),
    )(amp_slots, slot_tile, int_columns, amplitudes[0], ints)
    return jnp.swapaxes(result, 1, 2)[None]


def solution(mesh):
    nv = mesh.shape["vir"]
    nx = nv // min(4, nv)
    in_specs = (
        P(("occ", "vir"), None, None, None),
        P(("occ", "vir"), None),
        P("vir", "occ", None, None),
        P(),
        P(),
    )
    out_specs = P(("occ", "vir"), None, None, None)
    return jax.shard_map(
        functools.partial(body, nx), mesh=mesh, in_specs=in_specs, out_specs=out_specs,
        check_vma=False,
    )
```
